32 devices in a mesh: groups: 2 (over y), block: 4 (over x, core), tile: 4 (over z).
Axes of the slice: x: 2, y: 2, z: 4, core: 2. Of those that a mesh axis runs over, the one named last changes fastest.
Arguments:
- queries: float32 [8, 4, 16, 24, 1024], P(('groups', 'block'), 'tile'), parts along dimension 0
- keys: float32 [8, 4, 16, 24, 1024], P(('groups', 'block'), 'tile'), parts along dimension 0
- values: float32 [8, 4, 16, 24, 1024], P(('groups', 'block'), 'tile'), parts along dimension 0, may hold values from -6 to 6
- radii: int32 [4], replicated, may hold values from 1 to 4, as said below
Outputs:
- local_out: float32 [8, 4, 16, 24, 1024], P(('groups', 'block'), 'tile'), parts along dimension 0
- global_out: float32 [8, 4, 16, 24, 1024], P(('groups', 'block'), 'tile'), parts along dimension 0
The draws below stay inside these ranges and needn't reach their ends.
There are 2 independent parts, one for each index of `groups`. The reference program is written for one: setup_inputs(seed, part) draws one part's arguments, and reference() takes and returns one part's arrays. A program takes and returns all parts, laid end to end along the dimension named above; an argument that names none is the same for every part. Nothing has to cross between parts.
Inputs may be any that keep to these rules, and one draw needn't show every extreme that they name: `radii`: every head's radius is at least 1 and some head has radius 4.
All inputs are finite; a program needn't handle non-finite values.
Results may differ from the reference program's by a relative error of at most 0.0003.
Values sent between devices are 32-bit elements; how exact they have to be, the bound alone decides.
No kernel may reach another device: no remote copies, remote signals or barrier semaphores. Data moves between devices by JAX's collectives and lax.ppermute only.
A program may use at most 128 MiB of HBM per device.

```python
import math
import jax
import jax.numpy as jnp
from jax import lax

HEADS = 4
D = 1024
TILE_ROWS = 16
TILE_COLS = 24
R_MAX = 4
TILES = 4
GRID_C = 2
GRID_R = 2
HEIGHT = 32
WIDTH = 48
FRAMES = 4


def paired(key):
    base = jax.random.fold_in(key, 7)
    shape = (FRAMES, TILES, TILE_ROWS, TILE_COLS, D)
    query_draw = jnp.clip(jax.random.normal(jax.random.fold_in(base, 1), shape, jnp.float32), -5.0, 5.0)
    key_draw = jnp.clip(jax.random.normal(jax.random.fold_in(base, 2), shape, jnp.float32), -5.0, 5.0)
    return (query_draw, key_draw)


def draw_queries(key, part):
    return paired(key)[0]


def draw_keys(key, part):
    return paired(key)[1]


def draw_radii(key, part):
    chosen = jax.random.randint(jax.random.fold_in(key, 3), (HEADS,), 1, R_MAX + 1)
    widest = jax.random.randint(jax.random.fold_in(key, 4), (), 0, HEADS)
    return chosen.at[widest].set(R_MAX).astype(jnp.int32)


def block_scale(key, dims, shards, smallest, largest):
    factor_of, own = 1.0, jax.random.fold_in(key, 6)
    for dim, shards_of in shards:
        steps = jnp.exp(jax.random.uniform(jax.random.fold_in(own, dim), (shards_of,), jnp.float32, smallest / len(shards), largest / len(shards)))
        factor_of = factor_of * jnp.repeat(steps, dims[dim] // shards_of).reshape([-1 if axis == dim else 1 for axis in range(len(dims))])
    return factor_of


def normal_values(key, shape, spread, bound, shards=(), kind=jnp.bfloat16):
    array = jax.random.normal(key, shape, jnp.float32) * spread
    if len(shards) > 0:
        array = block_scale(key, shape, shards, -0.22, 0.18) * array
    return jnp.clip(array, min=-bound, max=bound).astype(kind)


def setup_inputs(seed: int = 0, part: int = 0) -> dict:
    key_list = jax.random.split(jax.random.key(seed), 5)
    own_keys = jax.random.split(jax.random.fold_in(key_list[4], part), 5)
    queries = draw_queries(jax.random.fold_in(jax.random.fold_in(key_list[4], part), 71), part)
    keys = draw_keys(jax.random.fold_in(jax.random.fold_in(key_list[4], part), 71), part)
    values = normal_values(own_keys[2], (FRAMES, TILES, TILE_ROWS, TILE_COLS, D), 1.0, 6.0, ((0, 4), (1, 4)), jnp.float32)
    radii = draw_radii(jax.random.fold_in(key_list[4], 71), part)
    return dict(queries=queries, keys=keys, values=values, radii=radii)


def neighborhood(query_tile, key_tile, value_tile, radii, row_start, col_start, height, width):
    rows, cols, dim = query_tile.shape
    head_count = radii.shape[0]
    head_dim = dim // head_count
    key_h = key_tile.shape[0]
    key_w = key_tile.shape[1]
    row_margin = (key_h - rows) // 2
    col_margin = (key_w - cols) // 2
    query_rows = query_tile.reshape(rows * cols, head_count, head_dim)
    key_rows = key_tile.reshape(key_h * key_w, head_count, head_dim)
    value_rows = value_tile.reshape(key_h * key_w, head_count, head_dim)
    scores = jnp.einsum('qhd,khd->hqk', query_rows, key_rows, precision=lax.Precision.HIGHEST) / math.sqrt(head_dim)
    query_pos = jnp.arange(rows * cols, dtype=jnp.int32)
    key_pos = jnp.arange(key_h * key_w, dtype=jnp.int32)
    query_row = query_pos // cols
    query_col = query_pos % cols
    key_row = key_pos // key_w - row_margin
    key_col = key_pos % key_w - col_margin
    reach = jnp.maximum(jnp.abs(query_row[:, None] - key_row[None, :]), jnp.abs(query_col[:, None] - key_col[None, :]))
    inside = (col_start + key_col >= 0) & (col_start + key_col < width) & (row_start + key_row >= 0) & (row_start + key_row < height)
    allowed = (reach[None, :, :] <= radii[:, None, None]) & inside[None, None, :]
    scores = jnp.where(allowed, scores, jnp.float32(-1e+30))
    top = lax.optimization_barrier(jnp.max(scores, axis=-1, keepdims=True))
    weights = jnp.exp(scores - top)
    weights = weights / lax.optimization_barrier(jnp.sum(weights, axis=-1, keepdims=True))
    result = jnp.einsum('hqk,khd->qhd', weights, value_rows, precision=lax.Precision.HIGHEST)
    return result.reshape(rows, cols, dim)

def linear_out(query_rows, state, zsum, vsum, count):
    head_dim = state.shape[1]
    feature = jax.nn.relu(query_rows)
    numer = jnp.einsum('qhd,hde->qhe', feature, state, precision=lax.Precision.HIGHEST) / math.sqrt(head_dim) + vsum[None, :, :]
    denom = jnp.einsum('qhd,hd->qh', feature, zsum, precision=lax.Precision.HIGHEST) / math.sqrt(head_dim) + count
    return numer / denom[:, :, None]

def to_frame(tiles):
    dim = tiles.shape[-1]
    placed = jnp.roll(tiles, 1, axis=0)
    grid = placed.reshape(GRID_R, GRID_C, TILE_ROWS, TILE_COLS, dim)
    return jnp.transpose(grid, (0, 2, 1, 3, 4)).reshape(HEIGHT, WIDTH, dim)

def reference(queries, keys, values, radii):
    frames = queries.shape[0]
    dim = queries.shape[-1]
    head_count = radii.shape[0]
    head_dim = dim // head_count
    local_list = []
    global_list = []
    state = jnp.zeros((head_count, head_dim, head_dim), jnp.float32)
    zsum = jnp.zeros((head_count, head_dim), jnp.float32)
    vsum = jnp.zeros((head_count, head_dim), jnp.float32)
    for frame in range(frames):
        pad_keys = jnp.pad(to_frame(keys[frame]), ((R_MAX, R_MAX), (R_MAX, R_MAX), (0, 0)))
        pad_values = jnp.pad(to_frame(values[frame]), ((R_MAX, R_MAX), (R_MAX, R_MAX), (0, 0)))
        frame_queries = queries[frame]

        def one_tile(tile_idx):
            position = ((tile_idx + 1) % TILES).astype(jnp.int32)
            row_start = (position // GRID_C * TILE_ROWS).astype(jnp.int32)
            col_start = (position % GRID_C * TILE_COLS).astype(jnp.int32)
            zero = jnp.zeros((), jnp.int32)
            sizes = (TILE_ROWS + 2 * R_MAX, TILE_COLS + 2 * R_MAX, dim)
            key_tile = lax.dynamic_slice(pad_keys, (row_start, col_start, zero), sizes)
            value_tile = lax.dynamic_slice(pad_values, (row_start, col_start, zero), sizes)
            query_tile = frame_queries[tile_idx]
            return neighborhood(query_tile, key_tile, value_tile, radii, row_start, col_start, HEIGHT, WIDTH)
        local_list.append(lax.map(one_tile, jnp.arange(TILES, dtype=jnp.int32)))
        key_rows = keys[frame].reshape(-1, head_count, head_dim)
        value_rows = values[frame].reshape(-1, head_count, head_dim)
        feature = jax.nn.relu(key_rows)
        state = state + jnp.einsum('khd,khe->hde', feature, value_rows, precision=lax.Precision.HIGHEST)
        zsum = zsum + lax.optimization_barrier(jnp.sum(feature, axis=0))
        vsum = vsum + lax.optimization_barrier(jnp.sum(value_rows, axis=0))
        count = jnp.float32((frame + 1) * HEIGHT * WIDTH)
        query_rows = queries[frame].reshape(-1, head_count, head_dim)
        global_list.append(linear_out(query_rows, state, zsum, vsum, count).reshape(queries.shape[1:]))
    return (jnp.stack(local_list), jnp.stack(global_list))
```

```python
import functools
import math

import jax
import jax.numpy as jnp
from jax import lax
from jax.experimental import pallas as pl
from jax.experimental.pallas import tpu as pltpu
from jax.sharding import PartitionSpec as P

R_MAX = 4
SUB = 8
EXACT = lax.Precision.HIGHEST
VMEM_LIMIT = 48 * 1024 * 1024


class Grid:
    def __init__(self, tiles, blocks):
        self.tiles = tiles
        self.blocks = blocks
        self.cols = min(4, tiles // 2)
        self.rows = tiles // self.cols
        self.col_sides = self.sides(self.cols)
        self.row_sides = self.sides(self.rows)

    @staticmethod
    def sides(count):
        return {1: (), 2: (0,)}.get(count, (-1, 1))

    @staticmethod
    def moved(place, side, count):
        if side == 0:
            return 1 - place
        there = place + side
        return there if 0 <= there < count else None

    def pairs(self, row_side, col_side):
        found = []
        for place in range(self.tiles):
            row, col = divmod(place, self.cols)
            if row_side is not None:
                row = self.moved(row, row_side, self.rows)
            if col_side is not None:
                col = self.moved(col, col_side, self.cols)
            if row is None or col is None:
                continue
            source = row * self.cols + col
            found.append(((source - 1) % self.tiles, (place - 1) % self.tiles))
        return found

    def place(self, tile):
        spot = lax.rem(tile + 1, self.tiles)
        return lax.div(spot, self.cols), lax.rem(spot, self.cols)

    @staticmethod
    def sends_high(place, side):
        return (place == 0) if side == 0 else (side == -1)

    @staticmethod
    def lies_after(place, side):
        return (place == 0) if side == 0 else (side == 1)

    @staticmethod
    def exists(place, side, count):
        if side == 0:
            return True
        return (place > 0) if side == -1 else (place < count - 1)


def pick(flag, yes, no):
    if isinstance(flag, bool):
        return yes if flag else no
    return jnp.where(flag, yes, no)


def whole(shape):
    return pl.BlockSpec(shape, lambda *_: (0,) * len(shape))


def pack_kernel(grid, heads, tile_ref, *refs):
    n_col, n_row = len(grid.col_sides), len(grid.row_sides)
    col_in = refs[: 2 * n_col]
    row_in = refs[2 * n_col : 2 * (n_col + n_row)]
    out = list(refs[2 * (n_col + n_row) :])
    row, col = grid.place(tile_ref[0])
    dim = (col_in + row_in)[0].shape[-1]
    head_dim = dim // heads
    for i, side in enumerate(grid.col_sides):
        high = grid.sends_high(col, side)
        target = out.pop(0)
        for kind in range(2):
            source = col_in[2 * i + kind].at[0, 0]
            for level in range(1, R_MAX + 1):
                line = pick(high, source[:, SUB - level, :], source[:, level - 1, :])
                for head in range(heads):
                    target[head * R_MAX + level - 1, kind] = line[
                        :, head * head_dim : (head + 1) * head_dim
                    ]
    for i, side in enumerate(grid.row_sides):
        high = grid.sends_high(row, side)
        target = out.pop(0)
        for kind in range(2):
            source = row_in[2 * i + kind].at[0, 0]
            for level in range(1, R_MAX + 1):
                at = pick(high, R_MAX - level, level - 1)
                line = source[at]
                for head in range(heads):
                    target[head * R_MAX + level - 1, kind] = line[
                        :, head * head_dim : (head + 1) * head_dim
                    ]
    for i, _ in enumerate(grid.row_sides):
        for side in grid.col_sides:
            high = grid.sends_high(col, side)
            target = out.pop(0)
            for kind in range(2):
                source = row_in[2 * i + kind].at[0, 0]
                cols = source.shape[1]
                for a in range(R_MAX):
                    target[kind, a * R_MAX : (a + 1) * R_MAX, :] = pick(
                        high, source[a, cols - R_MAX :, :], source[a, :R_MAX, :]
                    )


def pack(grid, tile, keys, values, heads):
    rows, cols, dim = keys.shape[2:]
    head_dim = dim // heads
    units = heads * R_MAX

    def col_map(side):
        def index(_, tile_ref):
            high = grid.sends_high(grid.place(tile_ref[0])[1], side)
            return (0, 0, 0, pick(high, cols // SUB - 1, 0), 0)

        return index

    def row_map(side):
        def index(_, tile_ref):
            high = grid.sends_high(grid.place(tile_ref[0])[0], side)
            return (0, 0, pick(high, rows // R_MAX - 1, 0), 0, 0)

        return index

    in_specs, operands, shapes = [], [], []
    for side in grid.col_sides:
        for array in (keys, values):
            in_specs.append(pl.BlockSpec((1, 1, rows, SUB, dim), col_map(side)))
            operands.append(array)
        shapes.append((units, 2, rows, head_dim))
    for side in grid.row_sides:
        for array in (keys, values):
            in_specs.append(pl.BlockSpec((1, 1, R_MAX, cols, dim), row_map(side)))
            operands.append(array)
        shapes.append((units, 2, cols, head_dim))
    for _ in grid.row_sides:
        for _ in grid.col_sides:
            shapes.append((2, R_MAX * R_MAX, dim))
    return pl.pallas_call(
        functools.partial(pack_kernel, grid, heads),
        name="pack_edges",
        out_shape=[jax.ShapeDtypeStruct(shape, jnp.float32) for shape in shapes],
        grid_spec=pltpu.PrefetchScalarGridSpec(
            num_scalar_prefetch=1,
            grid=(1,),
            in_specs=in_specs,
            out_specs=[whole(shape) for shape in shapes],
        ),
        compiler_params=pltpu.CompilerParams(vmem_limit_bytes=VMEM_LIMIT),
        cost_estimate=pl.CostEstimate(flops=0, transcendentals=0, bytes_accessed=6 << 20),
    )(tile, *operands)


def state_kernel(base_ref, key_ref, value_ref, out_ref):
    rows, cols, head_dim = key_ref.shape[2:]
    feature = jnp.maximum(key_ref[0, 0].reshape(rows * cols, head_dim), 0.0)
    value = value_ref[0, 0].reshape(rows * cols, head_dim)
    out_ref[0, :head_dim, :] = lax.dot_general(
        feature, value, (((0,), (0,)), ((), ())), precision=EXACT,
        preferred_element_type=jnp.float32,
    )
    line = lax.broadcasted_iota(jnp.int32, (SUB, head_dim), 0)
    vsum = jnp.sum(value, axis=0, keepdims=True)
    zsum = jnp.sum(feature, axis=0, keepdims=True)
    out_ref[0, head_dim:, :] = jnp.where(
        line == 0, vsum, jnp.where(line == 1, zsum, 0.0)
    )


def states(base, keys, values, heads, count):
    rows, cols, dim = keys.shape[2:]
    head_dim = dim // heads
    part = pl.BlockSpec(
        (1, 1, rows, cols, head_dim), lambda i, base_ref: (0, 0, 0, 0, base_ref[0] + i)
    )
    return pl.pallas_call(
        state_kernel,
        name="head_states",
        out_shape=jax.ShapeDtypeStruct((count, head_dim + SUB, head_dim), jnp.float32),
        grid_spec=pltpu.PrefetchScalarGridSpec(
            num_scalar_prefetch=1,
            grid=(count,),
            in_specs=[part, part],
            out_specs=pl.BlockSpec(
                (1, head_dim + SUB, head_dim), lambda i, base_ref: (i, 0, 0)
            ),
        ),
        compiler_params=pltpu.CompilerParams(vmem_limit_bytes=VMEM_LIMIT),
        cost_estimate=pl.CostEstimate(
            flops=count * 12 * rows * cols * head_dim * head_dim,
            transcendentals=0,
            bytes_accessed=count * 8 * rows * cols * head_dim,
        ),
    )(base, keys, values)


def global_kernel(tokens, aliased, base_ref, block_ref, query_ref, state_ref, *refs):
    out_ref = refs[-1]
    rows, cols, head_dim = query_ref.shape[2:]
    query = jnp.maximum(query_ref[0, 0].reshape(rows * cols, head_dim), 0.0)
    root = math.sqrt(head_dim)
    count = ((block_ref[0] + 1) * tokens).astype(jnp.float32)
    numer = (
        jnp.dot(
            query, state_ref[0, :head_dim, :], precision=EXACT,
            preferred_element_type=jnp.float32,
        )
        / root
        + state_ref[0, head_dim : head_dim + 1, :]
    )
    zsum = state_ref[0, head_dim + 1 : head_dim + 2, :]
    denom = jnp.sum(query * zsum, axis=1, keepdims=True) / root + count
    out_ref[0, 0] = (numer / denom).reshape(rows, cols, head_dim)


def global_part(base, block, queries, state, tokens, heads, onto=None):
    rows, cols, dim = queries.shape[2:]
    head_dim = dim // heads
    count = state.shape[0]
    part = pl.BlockSpec(
        (1, 1, rows, cols, head_dim),
        lambda i, base_ref, block_ref: (0, 0, 0, 0, base_ref[0] + i),
    )
    operands = [queries, state]
    in_specs = [
        part,
        pl.BlockSpec((1, head_dim + SUB, head_dim), lambda i, *_: (i, 0, 0)),
    ]
    aliases = {}
    if onto is not None:
        operands.append(onto)
        in_specs.append(pl.BlockSpec(memory_space=pl.ANY))
        aliases = {4: 0}
    return pl.pallas_call(
        functools.partial(global_kernel, tokens, onto is not None),
        name="global_heads",
        out_shape=jax.ShapeDtypeStruct(queries.shape, jnp.float32),
        grid_spec=pltpu.PrefetchScalarGridSpec(
            num_scalar_prefetch=2, grid=(count,), in_specs=in_specs, out_specs=part
        ),
        input_output_aliases=aliases,
        compiler_params=pltpu.CompilerParams(vmem_limit_bytes=VMEM_LIMIT),
        cost_estimate=pl.CostEstimate(
            flops=count * 12 * rows * cols * head_dim * head_dim,
            transcendentals=0,
            bytes_accessed=count * 8 * rows * cols * head_dim,
        ),
    )(base, block, *operands)


def divided(value, by):
    return ((value.astype(jnp.float32) + 0.5) * (1.0 / by)).astype(jnp.int32)


def local_kernel(grid, first, aliased, tile_ref, radii_ref, *refs):
    n_col, n_row = len(grid.col_sides), len(grid.row_sides)
    query_ref, key_ref, value_ref = refs[:3]
    col_in = refs[3 : 3 + n_col]
    row_in = refs[3 + n_col : 3 + n_col + n_row]
    corner_in = refs[3 + n_col + n_row : 3 + n_col + n_row + n_col * n_row]
    out_ref, reach_ref = refs[-2:]
    rows, cols, head_dim = query_ref.shape[2:]
    tokens = rows * cols

    @pl.when(pl.program_id(0) == 0)
    def _():
        row, col = grid.place(tile_ref[0])

        def span(count):
            return lax.broadcasted_iota(jnp.int32, (1, count), 1)

        index = span(tokens)
        key_row = [divided(index, cols)]
        key_col = [index - key_row[0] * cols]
        for side in grid.col_sides:
            after = grid.lies_after(col, side)
            there = grid.exists(col, side, grid.cols)
            index = span(R_MAX * rows)
            step = divided(index, rows)
            place = pick(after, cols + step, -1 - step)
            key_row.append(index - step * rows)
            key_col.append(pick(there, place, -(1 << 20)))
        for side in grid.row_sides:
            after = grid.lies_after(row, side)
            there = grid.exists(row, side, grid.rows)
            index = span(R_MAX * cols)
            step = divided(index, cols)
            place = pick(after, rows + step, -1 - step)
            key_row.append(pick(there, place, -(1 << 20)))
            key_col.append(index - step * cols)
        for row_side in grid.row_sides:
            for col_side in grid.col_sides:
                below = grid.lies_after(row, row_side)
                right = grid.lies_after(col, col_side)
                index = span(R_MAX * R_MAX)
                step = divided(index, R_MAX)
                place = pick(below, rows + step, step - R_MAX)
                there = grid.exists(row, row_side, grid.rows)
                key_row.append(pick(there, place, -(1 << 20)))
                step = index - step * R_MAX
                place = pick(right, cols + step, step - R_MAX)
                there = grid.exists(col, col_side, grid.cols)
                key_col.append(pick(there, place, -(1 << 20)))
        key_row = jnp.concatenate(key_row, axis=1)
        key_col = jnp.concatenate(key_col, axis=1)
        index = lax.broadcasted_iota(jnp.int32, (tokens, 1), 0)
        query_row = divided(index, cols)
        query_col = index - query_row * cols
        reach_ref[...] = jnp.maximum(
            jnp.abs(query_row - key_row), jnp.abs(query_col - key_col)
        )

    def gathered(own, kind):
        parts = [own[0, 0].reshape(tokens, head_dim)]
        parts += [ref[:, kind].reshape(R_MAX * rows, head_dim) for ref in col_in]
        parts += [ref[:, kind].reshape(R_MAX * cols, head_dim) for ref in row_in]
        parts += [ref[kind] for ref in corner_in]
        return jnp.concatenate(parts, axis=0)

    radius = radii_ref[first + pl.program_id(0)]
    query = query_ref[0, 0].reshape(tokens, head_dim)
    scores = lax.dot_general(
        query, gathered(key_ref, 0), (((1,), (1,)), ((), ())), precision=EXACT,
        preferred_element_type=jnp.float32,
    ) / math.sqrt(head_dim)
    scores = jnp.where(reach_ref[...] <= radius, scores, jnp.float32(-1e30))
    top = jnp.max(scores, axis=1, keepdims=True)
    weights = jnp.exp(scores - top)
    total = jnp.sum(weights, axis=1, keepdims=True)
    result = jnp.dot(
        weights, gathered(value_ref, 1), precision=EXACT,
        preferred_element_type=jnp.float32,
    )
    out_ref[0, 0] = (result / total).reshape(rows, cols, head_dim)


def local_part(grid, first, count, tile, radii, queries, keys, values, sides, onto=None):
    rows, cols, dim = queries.shape[2:]
    heads = radii.shape[0]
    head_dim = dim // heads
    part = pl.BlockSpec((1, 1, rows, cols, head_dim), lambda i, *_: (0, 0, 0, 0, first + i))
    col_in, row_in, corner_in = sides
    operands = [queries, keys, values, *col_in, *row_in, *corner_in]
    in_specs = [part] * 3
    for length, group in ((rows, col_in), (cols, row_in)):
        for array in group:
            start = first if array.shape[0] == heads * R_MAX else 0
            in_specs.append(
                pl.BlockSpec(
                    (R_MAX, 2, length, head_dim),
                    lambda i, *_, start=start: (start + i, 0, 0, 0),
                )
            )
    for _ in corner_in:
        in_specs.append(
            pl.BlockSpec((2, R_MAX * R_MAX, head_dim), lambda i, *_: (0, 0, first + i))
        )
    aliases = {}
    if onto is not None:
        aliases = {2 + len(operands): 0}
        operands.append(onto)
        in_specs.append(pl.BlockSpec(memory_space=pl.ANY))
    tokens = rows * cols
    held = (
        tokens
        + R_MAX * (rows * len(col_in) + cols * len(row_in))
        + R_MAX * R_MAX * len(corner_in)
    )
    return pl.pallas_call(
        functools.partial(local_kernel, grid, first, onto is not None),
        name="local_heads",
        out_shape=jax.ShapeDtypeStruct(queries.shape, jnp.float32),
        grid_spec=pltpu.PrefetchScalarGridSpec(
            num_scalar_prefetch=2,
            grid=(count,),
            in_specs=in_specs,
            out_specs=part,
            scratch_shapes=[pltpu.VMEM((tokens, held), jnp.int32)],
        ),
        input_output_aliases=aliases,
        compiler_params=pltpu.CompilerParams(vmem_limit_bytes=VMEM_LIMIT),
        cost_estimate=pl.CostEstimate(
            flops=count * 24 * tokens * held * head_dim,
            transcendentals=count * tokens * held,
            bytes_accessed=count * 16 * tokens * head_dim,
        ),
    )(tile, radii, *operands)


def swapped(value, axis, bit):
    count = lax.axis_size(axis)
    return lax.ppermute(value, axis, [(source, source ^ bit) for source in range(count)])


def bits(count, start=1):
    assert count & (count - 1) == 0
    bit = start
    while bit < count:
        yield bit
        bit *= 2


def body(queries, keys, values, radii):
    rows, cols, dim = queries.shape[2:]
    heads = radii.shape[0]
    grid = Grid(lax.axis_size("tile"), lax.axis_size("block"))
    tile_here = lax.axis_index("tile")
    block_here = lax.axis_index("block")
    tile = tile_here.astype(jnp.int32).reshape(1)
    block = block_here.astype(jnp.int32).reshape(1)

    packed = list(pack(grid, tile, keys, values, heads))
    col_in = [
        lax.ppermute(packed.pop(0), "tile", grid.pairs(None, side)) for side in grid.col_sides
    ]
    row_in = [
        lax.ppermute(packed.pop(0), "tile", grid.pairs(side, None)) for side in grid.row_sides
    ]
    corner_in = [
        lax.ppermute(packed.pop(0), "tile", grid.pairs(row_side, col_side))
        for row_side in grid.row_sides
        for col_side in grid.col_sides
    ]

    half = heads // 2
    odd = tile & 1
    own, other = odd * half, (1 - odd) * half
    sent = states(other, keys, values, heads, half)
    held = states(own, keys, values, heads, half) + swapped(sent, "tile", 1)
    total, before = held, None
    for bit in bits(grid.blocks):
        if 2 * bit < grid.blocks:
            arrived = swapped(total, "block", bit)
            total = total + arrived
            arrived = jnp.where(block_here & bit, arrived, 0.0)
        else:
            arrived = lax.ppermute(total, "block", [(k, k + bit) for k in range(bit)])
        before = arrived if before is None else before + arrived
    if before is not None:
        held = held + before
    for bit in bits(grid.tiles, 2):
        held = held + swapped(held, "tile", bit)
    tokens = grid.tiles * rows * cols
    global_out = global_part(own, block, queries, held, tokens, heads)
    rest = swapped(held, "tile", 1)
    global_out = global_part(other, block, queries, rest, tokens, heads, onto=global_out)

    sides = (col_in, row_in, corner_in)
    local_out = local_part(grid, 0, heads, tile, radii, queries, keys, values, sides)
    return local_out, global_out


def solution(mesh):
    split = P(("groups", "block"), "tile", None, None, None)
    return jax.shard_map(
        body,
        mesh=mesh,
        in_specs=(split, split, split, P()),
        out_specs=(split, split),
        check_vma=False,
    )
```

```python
import functools
import math

import jax
import jax.numpy as jnp
from jax import lax
from jax.experimental import pallas as pl
from jax.experimental.pallas import tpu as pltpu
from jax.sharding import PartitionSpec as P

R_MAX = 4
SUB = 8
VMEM_LIMIT = 22 * 1024 * 1024
LANES = 128
FAR = -(1 << 20)
EXACT = lax.Precision.HIGHEST


class Grid:
    def __init__(self, tiles):
        self.tiles = tiles
        self.cols = min(4, tiles // 2)
        self.rows = tiles // self.cols
        self.col_sides = self.sides(self.cols)
        self.row_sides = self.sides(self.rows)

    @staticmethod
    def sides(count):
        return {1: (), 2: (0,)}.get(count, (-1, 1))

    @staticmethod
    def moved(place, side, count):
        if side == 0:
            return 1 - place
        there = place + side
        return there if 0 <= there < count else None

    def pairs(self, row_side, col_side):
        found = []
        for place in range(self.tiles):
            row, col = divmod(place, self.cols)
            if row_side is not None:
                row = self.moved(row, row_side, self.rows)
            if col_side is not None:
                col = self.moved(col, col_side, self.cols)
            if row is None or col is None:
                continue
            source = row * self.cols + col
            found.append(((source - 1) % self.tiles, (place - 1) % self.tiles))
        return found

    def place(self, tile):
        spot = lax.rem(tile + 1, self.tiles)
        return lax.div(spot, self.cols), lax.rem(spot, self.cols)

    @staticmethod
    def sends_high(place, side):
        return (place == 0) if side == 0 else (side == -1)

    @staticmethod
    def lies_after(place, side):
        return (place == 0) if side == 0 else (side == 1)

    @staticmethod
    def exists(place, side, count):
        if side == 0:
            return True
        return (place > 0) if side == -1 else (place < count - 1)


def pick(flag, yes, no):
    if isinstance(flag, bool):
        return yes if flag else no
    return jnp.where(flag, yes, no)


def whole(shape):
    return pl.BlockSpec(shape, lambda *_: (0,) * len(shape))


class Units:
    def __init__(self, radii_ref, room):
        self.radii = [radii_ref[head] for head in range(radii_ref.shape[0])]
        self.heads = len(self.radii)
        self.room = room
        self.last = jnp.int32(0)
        for head in range(1, self.heads):
            self.last = jnp.where(self.radii[head] == R_MAX, head, self.last)

    def start(self, head):
        found = jnp.int32(0)
        for other in range(self.heads):
            ahead = (other < head) & (self.last != other)
            found += jnp.where(ahead, self.radii[other], 0)
        return jnp.where(self.last == head, self.room, found)

    def head_at(self, place):
        if isinstance(place, int) and place == self.heads - 1:
            return self.last
        return place + jnp.where(place >= self.last, 1, 0)


def pack_cols_kernel(grid, room, tile_ref, radii_ref, *refs):
    n_col = len(grid.col_sides)
    _, col = grid.place(tile_ref[0])
    units = Units(radii_ref, room)
    for i, side in enumerate(grid.col_sides):
        high = grid.sends_high(col, side)
        target = refs[2 * n_col + i]
        head_dim = target.shape[-1]
        target[...] = jnp.zeros(target.shape, target.dtype)
        for head in range(units.heads):
            start = units.start(head)
            part = slice(head * head_dim, (head + 1) * head_dim)
            for level in range(R_MAX):

                @pl.when(level < units.radii[head])
                def _(start=start, part=part, level=level, i=i, high=high, target=target):
                    for kind in range(2):
                        source = refs[2 * i + kind]
                        target[start + level, kind] = pick(
                            high,
                            source[0, 0, :, SUB - 1 - level, part],
                            source[0, 0, :, level, part],
                        )


def pack_rows_kernel(grid, room, tile_ref, radii_ref, *refs):
    n_row = len(grid.row_sides)
    row, col = grid.place(tile_ref[0])
    units = Units(radii_ref, room)
    out = list(refs[2 * n_row :])
    for i, side in enumerate(grid.row_sides):
        high = grid.sends_high(row, side)
        sources = refs[2 * i : 2 * i + 2]
        target, final = out.pop(0), out.pop(0)
        head_dim = target.shape[-1]
        target[...] = jnp.zeros(target.shape, target.dtype)
        for head in range(units.heads):
            start = units.start(head)
            part = slice(head * head_dim, (head + 1) * head_dim)
            is_last = units.last == head
            for level in range(R_MAX):
                line = pick(high, R_MAX - 1 - level, level)

                @pl.when((level < units.radii[head]) & jnp.logical_not(is_last))
                def _(start=start, part=part, level=level, line=line, target=target, sources=sources):
                    for kind in range(2):
                        target[start + level, kind] = sources[kind][0, 0, line, :, part]

                @pl.when(is_last)
                def _(part=part, level=level, line=line, final=final, sources=sources):
                    for kind in range(2):
                        final[level, kind] = sources[kind][0, 0, line, :, part]

    for i, _ in enumerate(grid.row_sides):
        for side in grid.col_sides:
            high = grid.sends_high(col, side)
            target = out.pop(0)
            for kind in range(2):
                source = refs[2 * i + kind].at[0, 0]
                cols = source.shape[1]
                for a in range(R_MAX):
                    target[kind, a * R_MAX : (a + 1) * R_MAX, :] = pick(
                        high, source[a, cols - R_MAX :, :], source[a, :R_MAX, :]
                    )


def packed(kernel, tile, radii, in_specs, operands, shapes, room):
    return pl.pallas_call(
        kernel,
        out_shape=[jax.ShapeDtypeStruct(shape, jnp.float32) for shape in shapes],
        grid_spec=pltpu.PrefetchScalarGridSpec(
            num_scalar_prefetch=2,
            grid=(1,),
            in_specs=in_specs,
            out_specs=[whole(shape) for shape in shapes],
        ),
        compiler_params=pltpu.CompilerParams(vmem_limit_bytes=room),
        cost_estimate=pl.CostEstimate(flops=0, transcendentals=0, bytes_accessed=4 << 20),
    )(tile, radii, *operands)


def pack_cols(grid, room, tile, radii, keys, values):
    rows, cols, dim = keys.shape[2:]
    heads = radii.shape[0]

    def index_map(side):
        def index(_, tile_ref, radii_ref):
            high = grid.sends_high(grid.place(tile_ref[0])[1], side)
            return (0, 0, 0, pick(high, cols // SUB - 1, 0), 0)

        return index

    in_specs, operands, shapes = [], [], []
    for side in grid.col_sides:
        for array in (keys, values):
            in_specs.append(pl.BlockSpec((1, 1, rows, SUB, dim), index_map(side)))
            operands.append(array)
        shapes.append((room + R_MAX, 2, rows, dim // heads))
    kernel = functools.partial(pack_cols_kernel, grid, room)
    return packed(kernel, tile, radii, in_specs, operands, shapes, VMEM_LIMIT)


def pack_rows(grid, room, tile, radii, keys, values):
    rows, cols, dim = keys.shape[2:]
    heads = radii.shape[0]

    def index_map(side):
        def index(_, tile_ref, radii_ref):
            high = grid.sends_high(grid.place(tile_ref[0])[0], side)
            return (0, 0, pick(high, rows // R_MAX - 1, 0), 0, 0)

        return index

    in_specs, operands, shapes = [], [], []
    for side in grid.row_sides:
        for array in (keys, values):
            in_specs.append(pl.BlockSpec((1, 1, R_MAX, cols, dim), index_map(side)))
            operands.append(array)
        shapes += [(units, 2, cols, dim // heads) for units in (room, R_MAX)]
    shapes += [(2, R_MAX * R_MAX, dim)] * (len(grid.row_sides) * len(grid.col_sides))
    kernel = functools.partial(pack_rows_kernel, grid, room)
    return packed(kernel, tile, radii, in_specs, operands, shapes, VMEM_LIMIT)


def state_kernel(sizes, which_ref, key_ref, value_ref, radii_ref, *out_refs):
    if sizes:
        *out_refs, place_ref = out_refs
        needed = sum(radii_ref[head] for head in range(radii_ref.shape[0])) - R_MAX
        place_ref[0] = sum((needed > size).astype(jnp.int32) for size in sizes[:-1])
    rows, cols, head_dim = key_ref.shape[2:]
    feature = jnp.maximum(key_ref[0, 0].reshape(rows * cols, head_dim), 0.0)
    value = value_ref[0, 0].reshape(rows * cols, head_dim)
    state = lax.dot_general(
        feature, value, (((0,), (0,)), ((), ())), precision=EXACT,
        preferred_element_type=jnp.float32,
    )
    line = lax.broadcasted_iota(jnp.int32, (SUB, head_dim), 0)
    vsum = jnp.sum(value, axis=0, keepdims=True)
    zsum = jnp.sum(feature, axis=0, keepdims=True)
    sums = jnp.where(line == 0, vsum, jnp.where(line == 1, zsum, 0.0))
    for i, out_ref in enumerate(out_refs):

        @pl.when(pl.program_id(0) == i)
        def _(out_ref=out_ref):
            out_ref[:head_dim, :] = state
            out_ref[head_dim:, :] = sums


def states(which, radii, keys, values, count, sizes=()):
    rows, cols, dim = keys.shape[2:]
    heads = radii.shape[0]
    head_dim = dim // heads
    part = pl.BlockSpec(
        (1, 1, rows, cols, head_dim),
        lambda i, which_ref: (0, 0, 0, 0, which_ref[0] * count + i),
    )
    shape = (head_dim + SUB, head_dim)
    kind = pltpu.HBM if sizes else jax.ShapeDtypeStruct
    out_shape = [kind(shape, jnp.float32)] * count
    out_specs = [whole(shape)] * count
    if sizes:
        out_shape.append(jax.ShapeDtypeStruct((1,), jnp.int32))
        out_specs.append(pl.BlockSpec(memory_space=pltpu.SMEM))
    return pl.pallas_call(
        functools.partial(state_kernel, sizes),
        name="head_states",
        out_shape=out_shape,
        grid_spec=pltpu.PrefetchScalarGridSpec(
            num_scalar_prefetch=1,
            grid=(count,),
            in_specs=[part, part, pl.BlockSpec(memory_space=pltpu.SMEM)],
            out_specs=out_specs,
        ),
        compiler_params=pltpu.CompilerParams(vmem_limit_bytes=VMEM_LIMIT),
        cost_estimate=pl.CostEstimate(
            flops=count * 12 * rows * cols * head_dim * head_dim,
            transcendentals=0,
            bytes_accessed=count * 8 * rows * cols * head_dim,
        ),
    )(which, keys, values, radii)


def global_kernel(tokens, count, head_ref, block_ref, query_ref, *refs):
    out_ref = refs[-1]
    rows, cols, head_dim = query_ref.shape[2:]
    query = jnp.maximum(query_ref[0, 0].reshape(rows * cols, head_dim), 0.0)
    root = math.sqrt(head_dim)
    seen = ((block_ref[0] + 1) * tokens).astype(jnp.float32)
    state = refs[0][...]
    for i in range(1, count):
        state = jnp.where(pl.program_id(0) == i, refs[i][...], state)
    numer = product(query, state[:head_dim]) / root + state[head_dim : head_dim + 1]
    zsum = state[head_dim + 1 : head_dim + 2]
    denom = jnp.sum(query * zsum, axis=1, keepdims=True) / root + seen
    out_ref[0, 0] = (numer / denom).reshape(rows, cols, head_dim)


def global_part(first, block, queries, parts, tokens, heads, onto=None):
    rows, cols, dim = queries.shape[2:]
    head_dim = dim // heads
    count = len(parts)
    part = pl.BlockSpec(
        (1, 1, rows, cols, head_dim),
        lambda i, first_ref, block_ref: (0, 0, 0, 0, first_ref[0] + i),
    )
    operands = [queries, *parts]
    in_specs = [part] + [whole(state.shape) for state in parts]
    aliases = {}
    if onto is not None:
        aliases = {2 + len(operands): 0}
        operands.append(onto)
        in_specs.append(pl.BlockSpec(memory_space=pl.ANY))
    return pl.pallas_call(
        functools.partial(global_kernel, tokens, count),
        out_shape=pltpu.HBM(queries.shape, jnp.float32),
        grid_spec=pltpu.PrefetchScalarGridSpec(
            num_scalar_prefetch=2, grid=(count,), in_specs=in_specs, out_specs=part
        ),
        input_output_aliases=aliases,
        compiler_params=pltpu.CompilerParams(vmem_limit_bytes=VMEM_LIMIT),
        cost_estimate=pl.CostEstimate(
            flops=count * 12 * rows * cols * head_dim * head_dim,
            transcendentals=0,
            bytes_accessed=count * 8 * rows * cols * head_dim,
        ),
    )(first, block, *operands)


def divided(value, by):
    return ((value.astype(jnp.float32) + 0.5) * (1.0 / by)).astype(jnp.int32)


def halves(value):
    high = value.astype(jnp.bfloat16)
    return high, (value - high.astype(jnp.float32)).astype(jnp.bfloat16)


def product(left, right):
    (left_high, left_low), (right_high, right_low) = halves(left), halves(right)
    one = functools.partial(jnp.dot, preferred_element_type=jnp.float32)
    return one(left_high, right_high) + (one(left_high, right_low) + one(left_low, right_high))


def scores_of(query, keys, reach, radius):
    scores = lax.dot_general(
        query * (1.0 / math.sqrt(query.shape[1])), keys, (((1,), (1,)), ((), ())),
        precision=EXACT, preferred_element_type=jnp.float32,
    )
    return jnp.where(reach <= radius, scores, jnp.float32(-1e30))


def span(count, axis=1):
    return lax.broadcasted_iota(jnp.int32, (1, count) if axis == 1 else (count, 1), axis)


def reach_of(query_row, query_col, key_row, key_col):
    key_row, key_col = (jnp.concatenate(part, axis=1) for part in (key_row, key_col))
    return jnp.maximum(jnp.abs(query_row - key_row), jnp.abs(query_col - key_col))


def inner_kernel(grid, room, takers, tile_ref, radii_ref, *refs):
    query_ref, key_ref, value_ref = refs[:3]
    sides = len(grid.row_sides)
    col_in = refs[3 : -3 - 2 * sides]
    out_ref, stats_ref, *edge_out, reach_ref = refs[-3 - 2 * sides :]
    rows, cols, head_dim = query_ref.shape[2:]
    tokens = rows * cols
    head = pl.program_id(0)

    @pl.when(head == 0)
    def _():
        _, col = grid.place(tile_ref[0])
        index = span(tokens)
        key_row = [divided(index, cols)]
        key_col = [index - key_row[0] * cols]
        for side in grid.col_sides:
            index = span(R_MAX * rows)
            away = divided(index, rows)
            place = pick(grid.lies_after(col, side), cols + away, -1 - away)
            key_row.append(index - away * rows)
            key_col.append(pick(grid.exists(col, side, grid.cols), place, FAR))
        index = span(tokens, 0)
        query_row = divided(index, cols)
        reach_ref[...] = reach_of(query_row, index - query_row * cols, key_row, key_col)

    units = pl.ds(Units(radii_ref, room).start(head), R_MAX)

    def gathered(own, kind):
        parts = [own[0, 0].reshape(tokens, head_dim)]
        left = list(col_in)
        for side_takers in takers:
            part = left.pop(0)[units, kind]
            for tiles in side_takers[1:]:
                mine = functools.reduce(jnp.logical_or, [tile_ref[0] == tile for tile in tiles])
                part = jnp.where(mine, left.pop(0)[units, kind], part)
            parts.append(part.reshape(R_MAX * rows, head_dim))
        return jnp.concatenate(parts, axis=0)

    query = query_ref[0, 0].reshape(tokens, head_dim)
    scores = scores_of(query, gathered(key_ref, 0), reach_ref[...], radii_ref[head])
    top = jnp.max(scores, axis=1, keepdims=True)
    weights = jnp.exp(scores - top)
    total = jnp.sum(weights, axis=1, keepdims=True)
    result = product(weights, gathered(value_ref, 1)) / total
    out_ref[0, 0] = result.reshape(rows, cols, head_dim)
    near = R_MAX * cols
    for i, side in enumerate(grid.row_sides):
        below = grid.lies_after(grid.place(tile_ref[0])[0], side)
        edge_out[2 * i][...] = pick(below, query[tokens - near :], query[:near])
        edge_out[2 * i + 1][...] = pick(below, result[tokens - near :], result[:near])
    lane = lax.broadcasted_iota(jnp.int32, stats_ref.shape, 1)
    stats_ref[...] = jnp.where(
        lane == 2 * head, top, jnp.where(lane == 2 * head + 1, total, stats_ref[...])
    )


def inner_part(grid, room, tile, radii, queries, keys, values, col_in):
    rows, cols, dim = queries.shape[2:]
    heads = radii.shape[0]
    head_dim = dim // heads
    part = pl.BlockSpec((1, 1, rows, cols, head_dim), lambda i, *_: (0, 0, 0, 0, i))
    takers = tuple(
        tuple(tuple(target for _, target in part) for part in apart(grid.pairs(None, side)).values())
        for side in grid.col_sides
    )
    tokens = rows * cols
    near = R_MAX * cols
    held = tokens + R_MAX * rows * len(grid.col_sides)
    return pl.pallas_call(
        functools.partial(inner_kernel, grid, room, takers),
        name="local_inner",
        out_shape=[
            pltpu.HBM(queries.shape, jnp.float32),
            jax.ShapeDtypeStruct((tokens, LANES), jnp.float32),
        ]
        + [jax.ShapeDtypeStruct((near, dim), jnp.float32)] * (2 * len(grid.row_sides)),
        grid_spec=pltpu.PrefetchScalarGridSpec(
            num_scalar_prefetch=2,
            grid=(heads,),
            in_specs=[part] * 3 + [whole(array.shape) for array in col_in],
            out_specs=[part, whole((tokens, LANES))]
            + [pl.BlockSpec((near, head_dim), lambda i, *_: (0, i))] * (2 * len(grid.row_sides)),
            scratch_shapes=[pltpu.VMEM((tokens, held), jnp.int32)],
        ),
        compiler_params=pltpu.CompilerParams(vmem_limit_bytes=VMEM_LIMIT),
        cost_estimate=pl.CostEstimate(
            flops=heads * 24 * tokens * held * head_dim,
            transcendentals=heads * tokens * held,
            bytes_accessed=heads * 16 * tokens * head_dim,
        ),
    )(tile, radii, queries, keys, values, *col_in)


def edge_kernel(grid, room, row_side, last, tile_ref, radii_ref, *refs):
    query_ref, row_ref = refs[:2]
    corner_in = refs[2 : 2 + len(grid.col_sides)]
    stats_ref, inner_ref = refs[2 + len(grid.col_sides) :][:2]
    out_ref = refs[-1]
    _, _, cols, head_dim = row_ref.shape
    near = R_MAX * cols
    units = Units(radii_ref, room)
    row, col = grid.place(tile_ref[0])
    below = grid.lies_after(row, row_side)
    there = grid.exists(row, row_side, grid.rows)
    index = span(near)
    away = divided(index, cols)
    key_row = [pick(there, pick(below, R_MAX + away, -1 - away), FAR)]
    key_col = [index - away * cols]
    for side in grid.col_sides:
        index = span(R_MAX * R_MAX)
        line = divided(index, R_MAX)
        key_row.append(pick(there, pick(below, R_MAX + line, line - R_MAX), FAR))
        line = index - line * R_MAX
        place = pick(grid.lies_after(col, side), cols + line, line - R_MAX)
        key_col.append(pick(grid.exists(col, side, grid.cols), place, FAR))
    index = span(near, 0)
    query_row = divided(index, cols)
    reach = reach_of(query_row, index - query_row * cols, key_row, key_col)
    lane = lax.broadcasted_iota(jnp.int32, stats_ref.shape, 1)
    if last:
        out_ref[...] = inner_ref[...]
    else:
        out_ref[0, 0] = inner_ref[...].reshape(out_ref.shape[2:])

    def add(place):
        head, start = units.last, 0
        if not last:
            head = units.head_at(place)
            start = units.start(head)
        part = pl.ds(pl.multiple_of(head * head_dim, LANES), head_dim)

        def gathered(kind):
            lines = [jnp.minimum(start + level, row_ref.shape[0] - 1) for level in range(R_MAX)]
            parts = [row_ref[line, kind] for line in lines]
            parts += [ref[kind, :, part] for ref in corner_in]
            return jnp.concatenate(parts, axis=0)

        scores = scores_of(query_ref[:, part], gathered(0), reach, radii_ref[head])
        stats = stats_ref[...]
        old_top = jnp.sum(jnp.where(lane == 2 * head, stats, 0.0), axis=1, keepdims=True)
        old_total = jnp.sum(jnp.where(lane == 2 * head + 1, stats, 0.0), axis=1, keepdims=True)
        top = jnp.maximum(old_top, jnp.max(scores, axis=1, keepdims=True))
        weights = jnp.exp(scores - top)
        old = old_total * jnp.exp(old_top - top)
        total = old + jnp.sum(weights, axis=1, keepdims=True)
        result = (inner_ref[:, part] * old + product(weights, gathered(1))) / total
        if last:
            out_ref[:, part] = result
        else:
            out_ref[0, 0, :, :, part] = result.reshape(R_MAX, cols, head_dim)

    for place in range(1 if last else units.heads - 1):
        add(place)


def edge_part(grid, room, row_side, tile, radii, query, row_in, corner_in, stats, inner, onto=None):
    near, dim = query.shape
    cols, head_dim = row_in.shape[2:]
    count = 1 if onto is None else radii.shape[0] - 1

    def lines(tile_ref):
        below = grid.lies_after(grid.place(tile_ref[0])[0], row_side)
        return pick(below, stats.shape[0] // near - 1, 0)

    operands = [query, row_in, *corner_in, stats, inner]
    in_specs = [whole(query.shape), whole(row_in.shape)]
    in_specs += [whole(array.shape) for array in corner_in]
    in_specs += [
        pl.BlockSpec((near, LANES), lambda i, tile_ref, _: (lines(tile_ref), 0)),
        whole(inner.shape),
    ]
    if onto is None:
        aliases = {}
        out_shape = jax.ShapeDtypeStruct(inner.shape, jnp.float32)
        out_specs = whole(inner.shape)
    else:
        aliases = {len(operands) + 2: 0}
        operands.append(onto)
        in_specs.append(pl.BlockSpec(memory_space=pl.ANY))
        out_shape = pltpu.HBM(onto.shape, jnp.float32)
        out_specs = pl.BlockSpec(
            (1, 1, R_MAX, cols, dim), lambda i, tile_ref, _: (0, 0, lines(tile_ref), 0, 0)
        )
    return pl.pallas_call(
        functools.partial(edge_kernel, grid, room, row_side, onto is None),
        out_shape=out_shape,
        grid_spec=pltpu.PrefetchScalarGridSpec(
            num_scalar_prefetch=2, grid=(1,), in_specs=in_specs, out_specs=out_specs
        ),
        input_output_aliases=aliases,
        compiler_params=pltpu.CompilerParams(vmem_limit_bytes=VMEM_LIMIT),
        cost_estimate=pl.CostEstimate(
            flops=count * 30 * near * near * head_dim,
            transcendentals=count * near * near,
            bytes_accessed=count * 24 * near * head_dim,
        ),
    )(tile, radii, *operands)


def apart(pairs):
    near = [pair for pair in pairs if abs(pair[0] - pair[1]) == 1]
    far = [pair for pair in pairs if abs(pair[0] - pair[1]) > 1]
    return {name: part for name, part in (("near", near), ("far", far)) if part}


def sent_apart(value, axis, pairs):
    return [lax.ppermute(value, axis, part) for part in apart(pairs).values()]


def swapped(value, axis, bit):
    count = lax.axis_size(axis)
    return lax.ppermute(value, axis, [(source, source ^ bit) for source in range(count)])


def bits(count, start=1):
    assert count & (count - 1) == 0
    bit = start
    while bit < count:
        yield bit
        bit *= 2


def block_sums(value, block):
    count = lax.axis_size("block")
    total, before = value, None
    for bit in bits(count):
        arrived = swapped(total, "block", bit)
        if 2 * bit < count:
            total = total + arrived
        arrived = jnp.where(block & bit, arrived, 0.0)
        before = arrived if before is None else before + arrived
    return value if before is None else value + before


def step(room, queries, keys, values, radii, *away):
    rows, cols, _ = queries.shape[2:]
    heads = radii.shape[0]
    tiles = lax.axis_size("tile")
    grid = Grid(tiles)
    block_here = lax.axis_index("block")
    tile = lax.axis_index("tile").astype(jnp.int32).reshape(1)
    block = block_here.astype(jnp.int32).reshape(1)

    cols_out = list(pack_cols(grid, room, tile, radii, keys, values))
    rows_out = list(pack_rows(grid, room, tile, radii, keys, values))
    col_in = []
    for side in grid.col_sides:
        col_in += sent_apart(cols_out.pop(0), "tile", grid.pairs(None, side))
    row_in = [
        [lax.ppermute(rows_out.pop(0), "tile", grid.pairs(side, None)) for _ in range(2)]
        for side in grid.row_sides
    ]
    corner_in = [
        lax.ppermute(rows_out.pop(0), "tile", grid.pairs(row_side, col_side))
        for row_side in grid.row_sides
        for col_side in grid.col_sides
    ]

    half = heads // 2
    own = tile & 1
    arrived = [swapped(part, "tile", 1) for part in away]
    held = [a + b for a, b in zip(states(own, radii, keys, values, half), arrived)]
    held = [block_sums(part, block_here) for part in held]
    for bit in bits(tiles, 2):
        held = [part + swapped(part, "tile", bit) for part in held]
    rest = [swapped(part, "tile", 1) for part in held]
    tokens = tiles * rows * cols
    global_out = global_part(own * half, block, queries, held, tokens, heads)
    for i, part in enumerate(rest):
        first = (1 - own) * half + i
        global_out = global_part(first, block, queries, [part], tokens, heads, onto=global_out)
    local_out, stats, *edges = inner_part(
        grid, room, tile, radii, queries, keys, values, col_in
    )
    for i, side in enumerate(grid.row_sides):
        corners = corner_in[i * len(grid.col_sides) : (i + 1) * len(grid.col_sides)]
        query, inner = edges[2 * i : 2 * i + 2]
        for group, onto in ((1, None), (0, local_out)):
            inner = edge_part(
                grid, room, side, tile, radii, query, row_in[i][group], corners, stats,
                inner, onto=onto,
            )
        local_out = inner
    return local_out, global_out


def rooms(heads):
    full = R_MAX * (heads - 1)
    return [-(-full * part // 12) for part in (6, 8, 10, 12)]


def solution(mesh):
    split = P(("groups", "block"), "tile", None, None, None)

    def body(queries, keys, values, radii):
        sizes = rooms(radii.shape[0])

        def branch(place):
            def run(*operands):
                return step(sizes[place], *operands)

            return run

        tile = lax.axis_index("tile").astype(jnp.int32).reshape(1)
        *away, place = states(
            1 - (tile & 1), radii, keys, values, radii.shape[0] // 2, sizes=tuple(sizes)
        )
        branches = [branch(place) for place, _ in enumerate(sizes)]
        return lax.switch(place[0], branches, queries, keys, values, radii, *away)

    return jax.shard_map(
        body,
        mesh=mesh,
        in_specs=(split, split, split, P()),
        out_specs=(split, split),
        check_vma=False,
    )
```
